128 devices in a mesh: grid: 8 (over y, core), dom: 16 (over x, z).
Axes of the slice: x: 4, y: 4, z: 4, core: 2. Of those that a mesh axis runs over, the one named last changes fastest.
Arguments:
- home: int32 [1024], P(('grid', 'dom')), may hold values from 0 to 1023, as said below
- p_grid: bfloat16 [1024, 5, 128, 128], P(('grid', 'dom')), may hold values from -0.25 to 0.25
- p_mask: int32 [1024, 5], P(('grid', 'dom')), may hold values 0 or 1
- h_grid: bfloat16 [1024, 5, 128, 128], P(('grid', 'dom')), may hold values from -0.25 to 0.25
- h_mask: int32 [1024, 5], P(('grid', 'dom')), may hold values 0 or 1
- x_inv: bfloat16 [1024, 5, 128, 128], P(('grid', 'dom')), may hold values from -1.1953125 to 1.1953125
- x_mask: int32 [1024, 5], P(('grid', 'dom')), may hold values 0 or 1
Outputs:
- density: bfloat16 [1024, 5, 128, 128], P(('grid', 'dom'))
- energy_density: bfloat16 [1024, 5, 128, 128], P(('grid', 'dom'))
The draws below stay inside these ranges and needn't reach their ends.
Inputs may be any that keep to these rules, and one draw needn't show every extreme that they name: home is a permutation of the block rows; each block row stays in its domain of 16 devices (128 rows), and one device of the grid layout sends at most ceil(8 / 16) rows to any one device of the domain layout, a count that is reached.
All inputs are finite; a program needn't handle non-finite values. No bound on the sum of `p_mask` or of `h_mask` or of `x_mask` on one device may be relied on, other than what follows from the above.
Results may differ from the reference program's by a relative error of at most 0.0065.
Values may be sent and summed in bfloat16 or wider, within the bound.
A program may use at most 128 MiB of HBM per device.

```python
import jax
import jax.numpy as jnp

BLOCK = 128
ROWS_DEV = 8
BLOCKS = 1024
DOMAINS = 8
GROUP = 16


def draw_home(key, part):
    first_key, second_key = jax.random.split(jax.random.fold_in(key, 11))
    source_keys = jax.random.split(first_key, DOMAINS * GROUP)
    target_keys = jax.random.split(second_key, DOMAINS * GROUP)
    ranks = jax.vmap(lambda one: jax.random.permutation(one, ROWS_DEV))(source_keys).reshape(DOMAINS, GROUP, ROWS_DEV).astype(jnp.int32)
    slots = jax.vmap(lambda one: jax.random.permutation(one, ROWS_DEV))(target_keys).reshape(DOMAINS, GROUP, ROWS_DEV).astype(jnp.int32)
    domain_ids = jnp.arange(DOMAINS, dtype=jnp.int32)[:, None, None]
    device_ids = jnp.arange(GROUP, dtype=jnp.int32)[None, :, None]
    target = (device_ids + ranks) % GROUP
    domain_full = jnp.broadcast_to(domain_ids, ranks.shape)
    slot = slots[domain_full, target, ranks]
    home = domain_ids * (GROUP * ROWS_DEV) + target * ROWS_DEV + slot
    return home.reshape(-1).astype(jnp.int32)


def set_ends(result, key, smallest, largest):
    extent = result.shape
    index_at = [jax.random.randint(jax.random.fold_in(key, axis), (), 0, extent[axis]) for axis in range(len(extent))]
    result = result.at[tuple(index_at)].set(smallest)
    longest = extent.index(max(extent))
    index_at[longest] = (index_at[longest] + 1) % extent[longest]
    return result.at[tuple(index_at)].set(largest)


def level_of(stream_key, extent, cuts, least, top_value):
    def one(dim, shards_of):
        heights = jax.random.uniform(jax.random.fold_in(jax.random.fold_in(stream_key, 6), dim), (shards_of,), jnp.float32, least / len(cuts), top_value / len(cuts))
        return jnp.repeat(jnp.exp(heights), extent[dim] // shards_of).reshape((-1,) + (1,) * (len(extent) - dim - 1))

    gain = one(*cuts[0])
    for cut in cuts[1:]:
        gain = gain * one(*cut)
    return gain


def scatter_about(rng, extent, deviation, most, shards=(), kind=jnp.bfloat16):
    result = jax.random.normal(rng, extent, jnp.float32) * deviation
    if len(shards) > 0:
        result = level_of(rng, extent, shards, -0.22, 0.18) * result
    return jnp.clip(result, min=-most, max=most).astype(kind)


def setup_inputs(seed: int = 0) -> dict:
    arg_keys = jax.random.split(jax.random.key(seed), 8)
    return {
        "home": draw_home(jax.random.fold_in(arg_keys[7], 71), 0),
        "p_grid": scatter_about(arg_keys[1], (BLOCKS, 5, BLOCK, BLOCK), (5 * BLOCK) ** -0.5, 0.25, ((0, 128),)),
        "p_mask": set_ends((jax.random.randint(arg_keys[2], (BLOCKS, 5), 0, 4) < 3).astype(jnp.int32), jax.random.fold_in(arg_keys[2], 1), 0, 1),
        "h_grid": scatter_about(arg_keys[3], (BLOCKS, 5, BLOCK, BLOCK), (5 * BLOCK) ** -0.5, 0.25, ((0, 128),)),
        "h_mask": set_ends((jax.random.randint(arg_keys[4], (BLOCKS, 5), 0, 4) < 3).astype(jnp.int32), jax.random.fold_in(arg_keys[4], 1), 0, 1),
        "x_inv": scatter_about(arg_keys[5], (BLOCKS, 5, BLOCK, BLOCK), 0.2, 1.1953125, ((0, 128),)),
        "x_mask": set_ends((jax.random.randint(arg_keys[6], (BLOCKS, 5), 0, 4) < 3).astype(jnp.int32), jax.random.fold_in(arg_keys[6], 1), 0, 1),
    }


def band_product(left, right, left_half, right_half, out_half, offset):
    count = left.shape[0]
    pieces = []
    for o in range(-out_half, out_half + 1):
        total = jnp.zeros((count, left.shape[2], right.shape[3]), jnp.float32)
        for a in range(-left_half, left_half + 1):
            b = o - a
            if -right_half <= b <= right_half:
                rows_b = right[offset + a: offset + a + count, b + right_half]
                total = total + jnp.einsum("nxy,nyz->nxz", left[:, a + left_half].astype(jnp.float32), rows_b.astype(jnp.float32))
        pieces.append(total)
    return jnp.stack(pieces, 1)


def padded(field, width):
    return jnp.pad(field, ((width, width), (0, 0), (0, 0), (0, 0)))


def reference(home, p_grid, p_mask, h_grid, h_mask, x_inv, x_mask):
    order = jnp.argsort(home).astype(jnp.int32)
    p_dom = (p_grid * p_mask[:, :, None, None].astype(jnp.bfloat16))[order]
    h_dom = (h_grid * h_mask[:, :, None, None].astype(jnp.bfloat16))[order]
    x_dom = x_inv * x_mask[:, :, None, None].astype(jnp.bfloat16)
    left_product = band_product(x_dom, padded(p_dom, 2), 2, 2, 4, 2).astype(jnp.bfloat16)
    right_product = band_product(p_dom, padded(x_dom, 2), 2, 2, 4, 2).astype(jnp.bfloat16)
    weighted = band_product(left_product, padded(h_dom, 4), 4, 2, 6, 4).astype(jnp.bfloat16)
    density = band_product(left_product, padded(x_dom, 4), 4, 2, 2, 4).astype(jnp.bfloat16)
    energy_density = band_product(weighted, padded(right_product, 6), 6, 4, 2, 6).astype(jnp.bfloat16)
    return density, energy_density
```

```python
import functools

import jax
import jax.numpy as jnp
from jax import lax
from jax.experimental import pallas as pl
from jax.experimental.pallas import tpu as pltpu
from jax.sharding import PartitionSpec as P

MESH = pl.DeviceIdType.MESH
BAND = 5
P_HALO, H_HALO, X_HALO = 6, 4, 4

P_PARTS = ((2, 2, 0, 5), (3, 1, 1, 4), (4, 1, 2, 3), (5, 1, 3, 2), (6, 1, 4, 1))
H_PARTS = ((4, 4, 0, 5),)
X_PARTS = ((1, 1, 1, 4), (2, 1, 2, 3), (3, 1, 3, 2), (4, 1, 4, 1))
PARTS = (P_PARTS, H_PARTS, X_PARTS)
HALOS = (P_HALO, H_HALO, X_HALO)


def kernel(
    domains,
    group,
    side,
    rows,
    home,
    p_mask,
    h_mask,
    x_mask,
    p_hbm,
    h_hbm,
    x_hbm,
    d_hbm,
    e_hbm,
    p_in,
    h_in,
    x_in,
    p_send,
    h_send,
    p_recv,
    h_recv,
    p_win,
    h_win,
    x_win,
    left,
    weighted,
    middle,
    d_out,
    e_out,
    meta_send,
    meta_recv,
    meta,
    local_sem,
    slot_send,
    slot_recv,
    halo_send,
    halo_recv,
    out_sem,
):
    g, t = lax.axis_index("grid"), lax.axis_index("dom")
    tx, tz = t // side, t % side
    block = p_in.shape[-1]
    me = g * group + t
    has_next, has_prev = me < domains * group - 1, me > 0
    after = lax.rem(me + 1, domains * group)
    before = lax.rem(me + domains * group - 1, domains * group)
    next_id = (after // group, after % group)
    prev_id = (before // group, before % group)

    def target(rel):
        return lax.rem(tx + rel // side, side) * side + lax.rem(tz + rel % side, side)

    loads = [
        pltpu.make_async_copy(src, dst, local_sem.at[i])
        for i, (src, dst) in enumerate(((p_hbm, p_in), (x_hbm, x_in), (h_hbm, h_in)))
    ]
    for load in loads:
        load.start()

    barrier = pltpu.get_barrier_semaphore()

    @pl.loop(1, group)
    def _(rel):
        pl.semaphore_signal(barrier, inc=1, device_id=(g, target(rel)), device_id_type=MESH)

    cross_next = (t == group - 1) & has_next
    cross_prev = (t == 0) & has_prev

    @pl.when(cross_next)
    def _():
        pl.semaphore_signal(barrier, inc=1, device_id=next_id, device_id_type=MESH)

    @pl.when(cross_prev)
    def _():
        pl.semaphore_signal(barrier, inc=1, device_id=prev_id, device_id_type=MESH)

    homes = [home[r] for r in range(rows)]
    devs = [(h // rows) % group for h in homes]
    lane = lax.broadcasted_iota(jnp.int32, (8, 128), 1)
    packed = jnp.zeros((8, 128), jnp.int32)
    for r in range(rows):
        packed = jnp.where(lane == r, homes[r], packed)
    meta_send[...] = packed
    meta_recv[0] = packed

    cross = cross_next.astype(jnp.int32) + cross_prev.astype(jnp.int32)
    pl.semaphore_wait(barrier, group - 1 + cross)

    def slot_copy(kind, src, dst, rel):
        return pltpu.make_async_remote_copy(
            src_ref=src,
            dst_ref=dst,
            send_sem=slot_send.at[kind, rel],
            recv_sem=slot_recv.at[kind, rel],
            device_id=(g, target(rel)),
            device_id_type=MESH,
        )

    def meta_copy(rel):
        return slot_copy(2, meta_send, meta_recv.at[rel], rel)

    def p_copy(rel):
        return slot_copy(0, p_send.at[rel], p_recv.at[rel], rel)

    def h_copy(rel):
        return slot_copy(1, h_send.at[rel], h_recv.at[rel], rel)

    def masked(ref, mask, row, b):
        scale = jnp.full((block, block), mask[row, b].astype(jnp.float32)).astype(jnp.bfloat16)
        return ref[row, b] * scale

    def fill(ref, mask, out, slot, rel):
        to = target(rel)
        row = jnp.int32(0)
        for r in range(rows):
            row = jnp.where(devs[r] == to, r, row)
        for b in range(BAND):
            out[slot, b] = masked(ref, mask, row, b)

    @pl.loop(1, group)
    def _(rel):
        meta_copy(rel).start()

    loads[0].wait()

    @pl.loop(1, group)
    def _(rel):
        fill(p_in, p_mask, p_send, rel, rel)
        p_copy(rel).start()

    fill(p_in, p_mask, p_recv, 0, 0)

    windows = (p_win, h_win, x_win)

    def halo_copies(m):
        win, halo = windows[m], HALOS[m]
        up, down = [], []
        for c, (far, n, b0, nb) in enumerate(PARTS[m]):
            low = halo + rows - far
            up.append(
                pltpu.make_async_remote_copy(
                    src_ref=win.at[pl.ds(low, n), pl.ds(b0, nb)],
                    dst_ref=win.at[pl.ds(low - rows, n), pl.ds(b0, nb)],
                    send_sem=halo_send.at[m, 0, c],
                    recv_sem=halo_recv.at[m, 0, c],
                    device_id=next_id,
                    device_id_type=MESH,
                )
            )
            high, b1 = halo + far - n, BAND - b0 - nb
            down.append(
                pltpu.make_async_remote_copy(
                    src_ref=win.at[pl.ds(high, n), pl.ds(b1, nb)],
                    dst_ref=win.at[pl.ds(high + rows, n), pl.ds(b1, nb)],
                    send_sem=halo_send.at[m, 1, c],
                    recv_sem=halo_recv.at[m, 1, c],
                    device_id=prev_id,
                    device_id_type=MESH,
                )
            )
        return up, down

    def start_halo(m):
        up, down = halo_copies(m)

        @pl.when(has_next)
        def _():
            for copy in up:
                copy.start()

        @pl.when(has_prev)
        def _():
            for copy in down:
                copy.start()

    def wait_halo(m):
        up, down = halo_copies(m)

        @pl.when(has_prev)
        def _():
            for copy in up:
                copy.wait_recv()

        @pl.when(has_next)
        def _():
            for copy in down:
                copy.wait_recv()

    def wait_halo_sent(m):
        up, down = halo_copies(m)

        @pl.when(has_next)
        def _():
            for copy in up:
                copy.wait_send()

        @pl.when(has_prev)
        def _():
            for copy in down:
                copy.wait_send()

    def clear(win, first, count):
        @pl.loop(first, first + count)
        def _(row):
            for b in range(BAND):
                win[row, b] = jnp.zeros((block, block), jnp.bfloat16)

    @pl.when(jnp.logical_not(has_prev))
    def _():
        for win, halo in zip(windows, HALOS):
            clear(win, 0, halo)

    @pl.when(jnp.logical_not(has_next))
    def _():
        for win, halo in zip(windows, HALOS):
            clear(win, halo + rows, halo)

    loads[1].wait()

    @pl.loop(0, rows)
    def _(row):
        for b in range(BAND):
            x_win[X_HALO + row, b] = masked(x_in, x_mask, row, b)

    start_halo(2)
    loads[2].wait()

    @pl.loop(1, group)
    def _(rel):
        fill(h_in, h_mask, h_send, rel, rel)
        h_copy(rel).start()

    fill(h_in, h_mask, h_recv, 0, 0)

    @pl.loop(1, group)
    def _(rel):
        meta_copy(rel).wait_recv()

    to_scalar = pltpu.make_async_copy(meta_recv, meta, local_sem.at[3])
    to_scalar.start()
    to_scalar.wait()

    def find(slot, found):
        for r in range(rows):
            value = meta[slot, 0, r]
            found = tuple(
                jnp.where(value == me * rows + j, slot, found[j]) for j in range(rows)
            )
        return found

    slots = lax.fori_loop(0, group, find, tuple(jnp.int32(0) for _ in range(rows)))

    def place(recv, win, halo):
        for j in range(rows):
            for b in range(BAND):
                win[halo + j, b] = recv[slots[j], b]

    @pl.loop(1, group)
    def _(rel):
        p_copy(rel).wait_recv()

    place(p_recv, p_win, P_HALO)
    start_halo(0)

    def piece(ref, halo, i, dr, dc):
        b = dc - dr + BAND // 2
        if 0 <= b < BAND:
            return ref[halo + 2 * i + dr, b]
        return jnp.zeros((block, block), jnp.bfloat16)

    def panel(ref, halo, i, o, low, high):
        return jnp.concatenate(
            [
                jnp.concatenate([piece(ref, halo, i, dr, 2 * o + c) for c in range(2)], 1)
                for dr in range(2 * low, 2 * high + 2)
            ],
            0,
        )

    def product(a, b):
        return jnp.dot(a, b, preferred_element_type=jnp.float32).astype(jnp.bfloat16)

    two = 2 * block

    def store(out, i, o, value):
        for r in range(2):
            for c in range(2):
                b = 2 * o + c - r + BAND // 2
                if 0 <= b < BAND:
                    out[2 * i + r, b] = value[
                        r * block : (r + 1) * block, c * block : (c + 1) * block
                    ]

    wait_halo(2)
    wait_halo(0)

    @pl.loop(0, rows // 2)
    def _(i):
        x_rows = jnp.concatenate(
            [
                jnp.concatenate([piece(x_win, X_HALO, i, r, dc) for dc in range(-2, 4)], 1)
                for r in range(2)
            ],
            0,
        )
        for o in range(-2, 3):
            low, high = max(-1, o - 1), min(1, o + 1)
            left[i, :, (o + 2) * two : (o + 3) * two] = product(
                x_rows[:, (low + 1) * two : (high + 2) * two],
                panel(p_win, P_HALO, i, o, low, high),
            )
        for o in range(-1, 2):
            store(
                d_out,
                i,
                o,
                product(
                    left[i, :, (o + 1) * two : (o + 4) * two],
                    panel(x_win, X_HALO, i, o, o - 1, o + 1),
                ),
            )

    d_copy = pltpu.make_async_copy(d_out, d_hbm, out_sem.at[0])
    d_copy.start()

    @pl.loop(1, group)
    def _(rel):
        h_copy(rel).wait_recv()

    place(h_recv, h_win, H_HALO)
    start_halo(1)
    wait_halo(1)

    @pl.loop(0, rows // 2)
    def _(i):
        for o in range(-3, 4):
            low, high = max(-2, o - 1), min(2, o + 1)
            weighted[:, (o + 3) * two : (o + 4) * two] = product(
                left[i, :, (low + 2) * two : (high + 3) * two],
                panel(h_win, H_HALO, i, o, low, high),
            )
        for o in range(-2, 3):
            middle[:, (o + 2) * two : (o + 3) * two] = product(
                weighted[:, (o + 2) * two : (o + 5) * two],
                panel(p_win, P_HALO, i, o, o - 1, o + 1),
            )
        for o in range(-1, 2):
            store(
                e_out,
                i,
                o,
                product(
                    middle[:, (o + 1) * two : (o + 4) * two],
                    panel(x_win, X_HALO, i, o, o - 1, o + 1),
                ),
            )

    e_copy = pltpu.make_async_copy(e_out, e_hbm, out_sem.at[1])
    e_copy.start()

    @pl.loop(1, group)
    def _(rel):
        meta_copy(rel).wait_send()
        p_copy(rel).wait_send()
        h_copy(rel).wait_send()

    for m in range(3):
        wait_halo_sent(m)
    d_copy.wait()
    e_copy.wait()


def solution(mesh):
    domains, group = mesh.shape["grid"], mesh.shape["dom"]
    side = 4

    def shards(home, p_grid, p_mask, h_grid, h_mask, x_inv, x_mask):
        rows, band, block, _ = p_grid.shape
        kind = p_grid.dtype
        two = 2 * block
        own = (rows, band, block, block)
        slots = (group, band, block, block)
        out = jax.ShapeDtypeStruct(own, kind)
        smem = pl.BlockSpec(memory_space=pltpu.SMEM)
        anywhere = pl.BlockSpec(memory_space=pl.ANY)
        return pl.pallas_call(
            functools.partial(kernel, domains, group, side, rows),
            out_shape=(out, out),
            in_specs=[smem] * 4 + [anywhere] * 3,
            out_specs=(anywhere, anywhere),
            scratch_shapes=[
                pltpu.VMEM(own, kind),
                pltpu.VMEM(own, kind),
                pltpu.VMEM(own, kind),
                pltpu.VMEM(slots, kind),
                pltpu.VMEM(slots, kind),
                pltpu.VMEM(slots, kind),
                pltpu.VMEM(slots, kind),
                pltpu.VMEM((rows + 2 * P_HALO, band, block, block), kind),
                pltpu.VMEM((rows + 2 * H_HALO, band, block, block), kind),
                pltpu.VMEM((rows + 2 * X_HALO, band, block, block), kind),
                pltpu.VMEM((rows // 2, two, 5 * two), kind),
                pltpu.VMEM((two, 7 * two), kind),
                pltpu.VMEM((two, 5 * two), kind),
                pltpu.VMEM(own, kind),
                pltpu.VMEM(own, kind),
                pltpu.VMEM((8, 128), jnp.int32),
                pltpu.VMEM((group, 8, 128), jnp.int32),
                pltpu.SMEM((group, 8, 128), jnp.int32),
                pltpu.SemaphoreType.DMA((4,)),
                pltpu.SemaphoreType.DMA((3, group)),
                pltpu.SemaphoreType.DMA((3, group)),
                pltpu.SemaphoreType.DMA((3, 2, 5)),
                pltpu.SemaphoreType.DMA((3, 2, 5)),
                pltpu.SemaphoreType.DMA((2,)),
            ],
            compiler_params=pltpu.CompilerParams(
                collective_id=0, has_side_effects=True, vmem_limit_bytes=48 << 20
            ),
        )(home, p_mask, h_mask, x_mask, p_grid, h_grid, x_inv)

    rows_spec = P(("grid", "dom"))
    return jax.shard_map(
        shards,
        mesh=mesh,
        in_specs=(rows_spec,) * 7,
        out_specs=(rows_spec, rows_spec),
        check_vma=False,
    )
```

```python
import functools

import jax
import jax.numpy as jnp
from jax import lax
from jax.experimental import pallas as pl
from jax.experimental.pallas import tpu as pltpu
from jax.sharding import PartitionSpec as P

MESH = pl.DeviceIdType.MESH
BAND = 5
P_HALO, H_HALO, X_HALO = 6, 4, 4

P_PARTS = ((2, 2, 0, 5), (3, 1, 1, 4), (4, 1, 2, 3), (5, 1, 3, 2), (6, 1, 4, 1))
H_PARTS = ((4, 4, 0, 5),)
X_PARTS = ((1, 1, 1, 4), (2, 1, 2, 3), (3, 1, 3, 2), (4, 1, 4, 1))
ORDER = (
    (1, 0), (0, 1), (3, 0), (0, 3), (2, 0), (0, 2), (1, 1), (3, 3),
    (1, 3), (3, 1), (2, 1), (2, 3), (1, 2), (3, 2), (2, 2),
)
PARTS = (P_PARTS, H_PARTS, X_PARTS)
HALOS = (P_HALO, H_HALO, X_HALO)


def kernel(
    domains,
    group,
    side,
    rows,
    home_hbm,
    p_mask_hbm,
    h_mask_hbm,
    x_mask_hbm,
    p_hbm,
    h_hbm,
    x_hbm,
    d_hbm,
    e_hbm,
    p_in,
    h_in,
    x_in,
    p_send,
    h_send,
    p_recv,
    h_recv,
    p_win,
    h_win,
    x_win,
    left,
    weighted,
    middle,
    d_out,
    e_out,
    meta_send,
    meta_recv,
    meta,
    home,
    p_mask,
    h_mask,
    x_mask,
    local_sem,
    slot_send,
    slot_recv,
    halo_send,
    halo_recv,
    out_sem,
):
    g, t = lax.axis_index("grid"), lax.axis_index("dom")
    tx, tz = t // side, t % side
    block = p_in.shape[-1]
    me = g * group + t
    has_next, has_prev = me < domains * group - 1, me > 0
    after = lax.rem(me + 1, domains * group)
    before = lax.rem(me + domains * group - 1, domains * group)
    next_id = (after // group, after % group)
    prev_id = (before // group, before % group)

    def target(rel):
        return lax.rem(tx + rel // side, side) * side + lax.rem(tz + rel % side, side)

    loads = [
        pltpu.make_async_copy(src, dst, local_sem.at[i])
        for i, (src, dst) in enumerate(
            (
                (home_hbm, home),
                (p_mask_hbm, p_mask),
                (p_hbm, p_in),
                (x_mask_hbm, x_mask),
                (x_hbm, x_in),
                (h_mask_hbm, h_mask),
                (h_hbm, h_in),
            )
        )
    ]
    for load in loads:
        load.start()

    barrier = pltpu.get_barrier_semaphore()

    @pl.loop(1, group)
    def _(rel):
        pl.semaphore_signal(barrier, inc=1, device_id=(g, target(rel)), device_id_type=MESH)

    cross_next = (t == group - 1) & has_next
    cross_prev = (t == 0) & has_prev

    @pl.when(cross_next)
    def _():
        pl.semaphore_signal(barrier, inc=1, device_id=next_id, device_id_type=MESH)

    @pl.when(cross_prev)
    def _():
        pl.semaphore_signal(barrier, inc=1, device_id=prev_id, device_id_type=MESH)

    loads[0].wait()
    homes = [home[r] for r in range(rows)]
    devs = [(h // rows) % group for h in homes]
    lane = lax.broadcasted_iota(jnp.int32, (8, 128), 1)
    packed = jnp.zeros((8, 128), jnp.int32)
    for r in range(rows):
        packed = jnp.where(lane == r, homes[r], packed)
    meta_send[...] = packed
    meta_recv[0] = packed

    cross = cross_next.astype(jnp.int32) + cross_prev.astype(jnp.int32)
    pl.semaphore_wait(barrier, group - 1 + cross)

    def slot_copy(kind, src, dst, rel):
        return pltpu.make_async_remote_copy(
            src_ref=src,
            dst_ref=dst,
            send_sem=slot_send.at[kind, rel],
            recv_sem=slot_recv.at[kind, rel],
            device_id=(g, target(rel)),
            device_id_type=MESH,
        )

    def meta_copy(rel):
        return slot_copy(2, meta_send, meta_recv.at[rel], rel)

    def p_copy(rel):
        return slot_copy(0, p_send.at[rel], p_recv.at[rel], rel)

    def h_copy(rel):
        return slot_copy(1, h_send.at[rel], h_recv.at[rel], rel)

    def masked(ref, mask, row, b):
        scale = jnp.full((block, block), mask[row, b].astype(jnp.float32)).astype(jnp.bfloat16)
        return ref[row, b] * scale

    def fill(ref, mask, out, slot, rel):
        to = target(rel)
        row = jnp.int32(0)
        for r in range(rows):
            row = jnp.where(devs[r] == to, r, row)
        for b in range(BAND):
            out[slot, b] = masked(ref, mask, row, b)

    @pl.loop(1, group)
    def _(rel):
        meta_copy(rel).start()

    order = [dx * side + dz for dx, dz in ORDER]
    loads[1].wait()
    loads[2].wait()
    for rel in order:
        fill(p_in, p_mask, p_send, rel, rel)
        p_copy(rel).start()

    fill(p_in, p_mask, p_recv, 0, 0)

    windows = (p_win, h_win, x_win)

    def halo_copies(m):
        win, halo = windows[m], HALOS[m]
        up, down = [], []
        for c, (far, n, b0, nb) in enumerate(PARTS[m]):
            low = halo + rows - far
            up.append(
                pltpu.make_async_remote_copy(
                    src_ref=win.at[pl.ds(low, n), pl.ds(b0, nb)],
                    dst_ref=win.at[pl.ds(low - rows, n), pl.ds(b0, nb)],
                    send_sem=halo_send.at[m, 0, c],
                    recv_sem=halo_recv.at[m, 0, c],
                    device_id=next_id,
                    device_id_type=MESH,
                )
            )
            high, b1 = halo + far - n, BAND - b0 - nb
            down.append(
                pltpu.make_async_remote_copy(
                    src_ref=win.at[pl.ds(high, n), pl.ds(b1, nb)],
                    dst_ref=win.at[pl.ds(high + rows, n), pl.ds(b1, nb)],
                    send_sem=halo_send.at[m, 1, c],
                    recv_sem=halo_recv.at[m, 1, c],
                    device_id=prev_id,
                    device_id_type=MESH,
                )
            )
        return up, down

    def start_halo(m):
        up, down = halo_copies(m)

        @pl.when(has_next)
        def _():
            for copy in up:
                copy.start()

        @pl.when(has_prev)
        def _():
            for copy in down:
                copy.start()

    def wait_halo(m):
        up, down = halo_copies(m)

        @pl.when(has_prev)
        def _():
            for copy in up:
                copy.wait_recv()

        @pl.when(has_next)
        def _():
            for copy in down:
                copy.wait_recv()

    def wait_halo_sent(m):
        up, down = halo_copies(m)

        @pl.when(has_next)
        def _():
            for copy in up:
                copy.wait_send()

        @pl.when(has_prev)
        def _():
            for copy in down:
                copy.wait_send()

    def clear(win, first, count):
        @pl.loop(first, first + count)
        def _(row):
            for b in range(BAND):
                win[row, b] = jnp.zeros((block, block), jnp.bfloat16)

    @pl.when(jnp.logical_not(has_prev))
    def _():
        for win, halo in zip(windows, HALOS):
            clear(win, 0, halo)

    @pl.when(jnp.logical_not(has_next))
    def _():
        for win, halo in zip(windows, HALOS):
            clear(win, halo + rows, halo)

    loads[3].wait()
    loads[4].wait()

    @pl.loop(0, rows)
    def _(row):
        for b in range(BAND):
            x_win[X_HALO + row, b] = masked(x_in, x_mask, row, b)

    start_halo(2)
    loads[5].wait()
    loads[6].wait()
    for rel in order:
        fill(h_in, h_mask, h_send, rel, rel)
        h_copy(rel).start()

    fill(h_in, h_mask, h_recv, 0, 0)

    @pl.loop(1, group)
    def _(rel):
        meta_copy(rel).wait_recv()

    to_scalar = pltpu.make_async_copy(meta_recv, meta, local_sem.at[7])
    to_scalar.start()
    to_scalar.wait()

    def find(slot, found):
        for r in range(rows):
            value = meta[slot, 0, r]
            found = tuple(
                jnp.where(value == me * rows + j, slot, found[j]) for j in range(rows)
            )
        return found

    slots = lax.fori_loop(0, group, find, tuple(jnp.int32(0) for _ in range(rows)))

    def place(recv, win, halo):
        for j in range(rows):
            for b in range(BAND):
                win[halo + j, b] = recv[slots[j], b]

    @pl.loop(1, group)
    def _(rel):
        p_copy(rel).wait_recv()

    place(p_recv, p_win, P_HALO)
    start_halo(0)

    def piece(ref, halo, i, dr, dc):
        b = dc - dr + BAND // 2
        if 0 <= b < BAND:
            return ref[halo + 2 * i + dr, b]
        return jnp.zeros((block, block), jnp.bfloat16)

    def panel(ref, halo, i, o, low, high):
        return jnp.concatenate(
            [
                jnp.concatenate([piece(ref, halo, i, dr, 2 * o + c) for c in range(2)], 1)
                for dr in range(2 * low, 2 * high + 2)
            ],
            0,
        )

    def product(a, b):
        return jnp.dot(a, b, preferred_element_type=jnp.float32).astype(jnp.bfloat16)

    two = 2 * block

    def store(out, i, o, value):
        for r in range(2):
            for c in range(2):
                b = 2 * o + c - r + BAND // 2
                if 0 <= b < BAND:
                    out[2 * i + r, b] = value[
                        r * block : (r + 1) * block, c * block : (c + 1) * block
                    ]

    wait_halo(2)
    wait_halo(0)

    @pl.loop(0, rows // 2)
    def _(i):
        x_rows = jnp.concatenate(
            [
                jnp.concatenate([piece(x_win, X_HALO, i, r, dc) for dc in range(-2, 4)], 1)
                for r in range(2)
            ],
            0,
        )
        for o in range(-2, 3):
            low, high = max(-1, o - 1), min(1, o + 1)
            left[i, :, (o + 2) * two : (o + 3) * two] = product(
                x_rows[:, (low + 1) * two : (high + 2) * two],
                panel(p_win, P_HALO, i, o, low, high),
            )
        for o in range(-1, 2):
            store(
                d_out,
                i,
                o,
                product(
                    left[i, :, (o + 1) * two : (o + 4) * two],
                    panel(x_win, X_HALO, i, o, o - 1, o + 1),
                ),
            )

    d_copy = pltpu.make_async_copy(d_out, d_hbm, out_sem.at[0])
    d_copy.start()

    @pl.loop(1, group)
    def _(rel):
        h_copy(rel).wait_recv()

    place(h_recv, h_win, H_HALO)
    start_halo(1)
    wait_halo(1)

    @pl.loop(0, rows // 2)
    def _(i):
        for o in range(-3, 4):
            low, high = max(-2, o - 1), min(2, o + 1)
            weighted[:, (o + 3) * two : (o + 4) * two] = product(
                left[i, :, (low + 2) * two : (high + 3) * two],
                panel(h_win, H_HALO, i, o, low, high),
            )
        for o in range(-2, 3):
            middle[:, (o + 2) * two : (o + 3) * two] = product(
                weighted[:, (o + 2) * two : (o + 5) * two],
                panel(p_win, P_HALO, i, o, o - 1, o + 1),
            )
        for o in range(-1, 2):
            store(
                e_out,
                i,
                o,
                product(
                    middle[:, (o + 1) * two : (o + 4) * two],
                    panel(x_win, X_HALO, i, o, o - 1, o + 1),
                ),
            )

    e_copy = pltpu.make_async_copy(e_out, e_hbm, out_sem.at[1])
    e_copy.start()

    @pl.loop(1, group)
    def _(rel):
        meta_copy(rel).wait_send()
        p_copy(rel).wait_send()
        h_copy(rel).wait_send()

    for m in range(3):
        wait_halo_sent(m)
    d_copy.wait()
    e_copy.wait()


def solution(mesh):
    domains, group = mesh.shape["grid"], mesh.shape["dom"]
    side = 4

    def shards(home, p_grid, p_mask, h_grid, h_mask, x_inv, x_mask):
        rows, band, block, _ = p_grid.shape
        kind = p_grid.dtype
        two = 2 * block
        own = (rows, band, block, block)
        slots = (group, band, block, block)
        out = jax.ShapeDtypeStruct(own, kind)
        anywhere = pl.BlockSpec(memory_space=pl.ANY)
        return pl.pallas_call(
            functools.partial(kernel, domains, group, side, rows),
            out_shape=(out, out),
            in_specs=[anywhere] * 7,
            out_specs=(anywhere, anywhere),
            scratch_shapes=[
                pltpu.VMEM(own, kind),
                pltpu.VMEM(own, kind),
                pltpu.VMEM(own, kind),
                pltpu.VMEM(slots, kind),
                pltpu.VMEM(slots, kind),
                pltpu.VMEM(slots, kind),
                pltpu.VMEM(slots, kind),
                pltpu.VMEM((rows + 2 * P_HALO, band, block, block), kind),
                pltpu.VMEM((rows + 2 * H_HALO, band, block, block), kind),
                pltpu.VMEM((rows + 2 * X_HALO, band, block, block), kind),
                pltpu.VMEM((rows // 2, two, 5 * two), kind),
                pltpu.VMEM((two, 7 * two), kind),
                pltpu.VMEM((two, 5 * two), kind),
                pltpu.VMEM(own, kind),
                pltpu.VMEM(own, kind),
                pltpu.VMEM((8, 128), jnp.int32),
                pltpu.VMEM((group, 8, 128), jnp.int32),
                pltpu.SMEM((group, 8, 128), jnp.int32),
                pltpu.SMEM((rows,), jnp.int32),
                pltpu.SMEM((rows, band), jnp.int32),
                pltpu.SMEM((rows, band), jnp.int32),
                pltpu.SMEM((rows, band), jnp.int32),
                pltpu.SemaphoreType.DMA((8,)),
                pltpu.SemaphoreType.DMA((3, group)),
                pltpu.SemaphoreType.DMA((3, group)),
                pltpu.SemaphoreType.DMA((3, 2, 5)),
                pltpu.SemaphoreType.DMA((3, 2, 5)),
                pltpu.SemaphoreType.DMA((2,)),
            ],
            compiler_params=pltpu.CompilerParams(
                collective_id=0, has_side_effects=True, vmem_limit_bytes=60 << 20
            ),
        )(home, p_mask, h_mask, x_mask, p_grid, h_grid, x_inv)

    rows_spec = P(("grid", "dom"))
    return jax.shard_map(
        shards,
        mesh=mesh,
        in_specs=(rows_spec,) * 7,
        out_specs=(rows_spec, rows_spec),
        check_vma=False,
    )
```

```python
import functools

import jax
import jax.numpy as jnp
from jax import lax
from jax.experimental import pallas as pl
from jax.experimental.pallas import tpu as pltpu
from jax.sharding import PartitionSpec as P

MESH = pl.DeviceIdType.MESH
BAND = 5
P_HALO, H_HALO, X_HALO = 6, 4, 4

P_PARTS = ((2, 2, 0, 5), (3, 1, 1, 4), (4, 1, 2, 3), (5, 1, 3, 2), (6, 1, 4, 1))
H_CUTS = ((0, 3), (3, 2))
H_PARTS = tuple((4, 4, b0, nb) for b0, nb in H_CUTS)
X_PARTS = ((1, 1, 1, 4), (2, 1, 2, 3), (3, 1, 3, 2), (4, 1, 4, 1))
ORDER = (
    (1, 0), (0, 1), (3, 0), (0, 3), (2, 0), (0, 2), (1, 1), (3, 3),
    (1, 3), (3, 1), (2, 1), (2, 3), (1, 2), (3, 2), (2, 2),
)
PARTS = (P_PARTS, H_PARTS, X_PARTS)
HALOS = (P_HALO, H_HALO, X_HALO)


def kernel(
    domains,
    group,
    side,
    rows,
    home_hbm,
    p_mask_hbm,
    h_mask_hbm,
    x_mask_hbm,
    p_hbm,
    h_hbm,
    x_hbm,
    d_hbm,
    e_hbm,
    p_in,
    h_in,
    x_in,
    p_send,
    h_send,
    p_recv,
    h_recv_0,
    h_recv_1,
    p_win,
    h_win,
    x_win,
    factors,
    weighted,
    d_out,
    e_out,
    meta_send,
    meta_recv,
    meta,
    home,
    p_mask,
    h_mask,
    x_mask,
    local_sem,
    slot_send,
    slot_recv,
    halo_send,
    halo_recv,
    out_sem,
):
    g, t = lax.axis_index("grid"), lax.axis_index("dom")
    tx, tz = t // side, t % side
    block = p_in.shape[-1]
    me = g * group + t
    has_next, has_prev = me < domains * group - 1, me > 0
    after = lax.rem(me + 1, domains * group)
    before = lax.rem(me + domains * group - 1, domains * group)
    next_id = (after // group, after % group)
    prev_id = (before // group, before % group)

    def target(rel):
        return lax.rem(tx + rel // side, side) * side + lax.rem(tz + rel % side, side)

    loads = [
        pltpu.make_async_copy(src, dst, local_sem.at[i])
        for i, (src, dst) in enumerate(
            (
                (home_hbm, home),
                (p_mask_hbm, p_mask),
                (p_hbm, p_in),
                (x_mask_hbm, x_mask),
                (x_hbm, x_in),
                (h_mask_hbm, h_mask),
                (h_hbm, h_in),
            )
        )
    ]
    for load in loads:
        load.start()

    barrier = pltpu.get_barrier_semaphore()

    @pl.loop(1, group)
    def _(rel):
        pl.semaphore_signal(barrier, inc=1, device_id=(g, target(rel)), device_id_type=MESH)

    cross_next = (t == group - 1) & has_next
    cross_prev = (t == 0) & has_prev

    @pl.when(cross_next)
    def _():
        pl.semaphore_signal(barrier, inc=1, device_id=next_id, device_id_type=MESH)

    @pl.when(cross_prev)
    def _():
        pl.semaphore_signal(barrier, inc=1, device_id=prev_id, device_id_type=MESH)

    loads[0].wait()
    homes = [home[r] for r in range(rows)]
    devs = [(h // rows) % group for h in homes]
    lane = lax.broadcasted_iota(jnp.int32, (8, 128), 1)
    packed = jnp.zeros((8, 128), jnp.int32)
    for r in range(rows):
        packed = jnp.where(lane == r, homes[r], packed)
    meta_send[...] = packed
    meta_recv[0] = packed

    def slot_copy(kind, src, dst, rel):
        return pltpu.make_async_remote_copy(
            src_ref=src,
            dst_ref=dst,
            send_sem=slot_send.at[kind, rel],
            recv_sem=slot_recv.at[kind, rel],
            device_id=(g, target(rel)),
            device_id_type=MESH,
        )

    def meta_copy(rel):
        return slot_copy(2, meta_send, meta_recv.at[rel], rel)

    def p_copy(rel):
        return slot_copy(0, p_send.at[rel], p_recv.at[rel], rel)

    h_recv = (h_recv_0, h_recv_1)

    def h_copy(rel, part):
        cut = pl.ds(*H_CUTS[part])
        return slot_copy((1, 3)[part], h_send.at[rel, cut], h_recv[part].at[rel], rel)

    def masked(ref, mask, row, b):
        scale = jnp.full((block, block), mask[row, b].astype(jnp.float32)).astype(jnp.bfloat16)
        return ref[row, b] * scale

    def fill(ref, mask, out, slot, rel, first=0, count=BAND):
        to = target(rel)
        row = jnp.int32(0)
        for r in range(rows):
            row = jnp.where(devs[r] == to, r, row)
        for b in range(count):
            out[slot, b] = masked(ref, mask, row, first + b)

    order = [dx * side + dz for dx, dz in ORDER]
    loads[1].wait()
    loads[2].wait()
    for rel in order:
        fill(p_in, p_mask, p_send, rel, rel)

    cross = cross_next.astype(jnp.int32) + cross_prev.astype(jnp.int32)
    pl.semaphore_wait(barrier, group - 1 + cross)

    @pl.loop(1, group)
    def _(rel):
        meta_copy(rel).start()

    for rel in order:
        p_copy(rel).start()

    fill(p_in, p_mask, p_recv, 0, 0)

    windows = (p_win, h_win, x_win)

    def halo_copies(m):
        win, halo = windows[m], HALOS[m]
        up, down = [], []
        for c, (far, n, b0, nb) in enumerate(PARTS[m]):
            low = halo + rows - far
            up.append(
                pltpu.make_async_remote_copy(
                    src_ref=win.at[pl.ds(low, n), pl.ds(b0, nb)],
                    dst_ref=win.at[pl.ds(low - rows, n), pl.ds(b0, nb)],
                    send_sem=halo_send.at[m, 0, c],
                    recv_sem=halo_recv.at[m, 0, c],
                    device_id=next_id,
                    device_id_type=MESH,
                )
            )
            high, b1 = halo + far - n, b0 if m == 1 else BAND - b0 - nb
            down.append(
                pltpu.make_async_remote_copy(
                    src_ref=win.at[pl.ds(high, n), pl.ds(b1, nb)],
                    dst_ref=win.at[pl.ds(high + rows, n), pl.ds(b1, nb)],
                    send_sem=halo_send.at[m, 1, c],
                    recv_sem=halo_recv.at[m, 1, c],
                    device_id=prev_id,
                    device_id_type=MESH,
                )
            )
        return up, down

    def start_halo(m, parts=None):
        up, down = halo_copies(m)
        for c in range(len(up)) if parts is None else parts:
            pl.when(has_next)(up[c].start)
            pl.when(has_prev)(down[c].start)

    def wait_halo(m):
        up, down = halo_copies(m)

        @pl.when(has_prev)
        def _():
            for copy in up:
                copy.wait_recv()

        @pl.when(has_next)
        def _():
            for copy in down:
                copy.wait_recv()

    def wait_halo_sent(m):
        up, down = halo_copies(m)

        @pl.when(has_next)
        def _():
            for copy in up:
                copy.wait_send()

        @pl.when(has_prev)
        def _():
            for copy in down:
                copy.wait_send()

    def clear(win, first, count):
        @pl.loop(first, first + count)
        def _(row):
            for b in range(BAND):
                win[row, b] = jnp.zeros((block, block), jnp.bfloat16)

    loads[3].wait()
    loads[4].wait()

    @pl.loop(0, rows)
    def _(row):
        for b in range(BAND):
            x_win[X_HALO + row, b] = masked(x_in, x_mask, row, b)

    loads[5].wait()
    loads[6].wait()
    for rel in order:
        fill(h_in, h_mask, h_send, rel, rel)
        h_copy(rel, 0).start()
    for rel in order:
        h_copy(rel, 1).start()

    for recv, cut in zip(h_recv, H_CUTS):
        fill(h_in, h_mask, recv, 0, 0, *cut)

    @pl.when(jnp.logical_not(has_prev))
    def _():
        for win, halo in zip(windows, HALOS):
            clear(win, 0, halo)

    @pl.when(jnp.logical_not(has_next))
    def _():
        for win, halo in zip(windows, HALOS):
            clear(win, halo + rows, halo)

    @pl.loop(1, group)
    def _(rel):
        meta_copy(rel).wait_recv()

    to_scalar = pltpu.make_async_copy(meta_recv.at[:, pl.ds(0, 1)], meta, local_sem.at[7])
    to_scalar.start()
    to_scalar.wait()

    def find(slot, found):
        for r in range(rows):
            value = meta[slot, 0, r]
            found = tuple(
                jnp.where(value == me * rows + j, slot, found[j]) for j in range(rows)
            )
        return found

    slots = lax.fori_loop(0, group, find, tuple(jnp.int32(0) for _ in range(rows)))

    def place(recv, win, halo, first=0, count=BAND):
        for j in range(rows):
            for b in range(count):
                win[halo + j, first + b] = recv[slots[j], b]

    @pl.loop(1, group)
    def _(rel):
        p_copy(rel).wait_recv()

    place(p_recv, p_win, P_HALO)
    start_halo(0)

    def piece(ref, halo, i, dr, dc):
        b = dc - dr + BAND // 2
        if 0 <= b < BAND:
            return ref[halo + 2 * i + dr, b]
        return jnp.zeros((block, block), jnp.bfloat16)

    def panel(ref, halo, i, o, low, high):
        return jnp.concatenate(
            [
                jnp.concatenate([piece(ref, halo, i, dr, 2 * o + c) for c in range(2)], 1)
                for dr in range(2 * low, 2 * high + 2)
            ],
            0,
        )

    def product(a, b):
        return jnp.dot(a, b, preferred_element_type=jnp.float32).astype(jnp.bfloat16)

    two = 2 * block

    def store(out, i, o, value):
        for r in range(2):
            for c in range(2):
                b = 2 * o + c - r + BAND // 2
                if 0 <= b < BAND:
                    out[2 * i + r, b] = value[
                        r * block : (r + 1) * block, c * block : (c + 1) * block
                    ]

    for part, cut in enumerate(H_CUTS):

        @pl.loop(1, group)
        def _(rel):
            h_copy(rel, part).wait_recv()

        place(h_recv[part], h_win, H_HALO, *cut)
        start_halo(1, (part,))

    start_halo(2)
    wait_halo(0)

    @pl.loop(0, rows // 2)
    def _(i):
        x_rows = jnp.concatenate(
            [
                jnp.concatenate([piece(x_win, X_HALO, i, r, dc) for dc in range(-2, 4)], 1)
                for r in range(2)
            ],
            0,
        )
        for o in range(-2, 3):
            low, high = max(-1, o - 1), min(1, o + 1)
            factors[i, pl.ds(0, two), (o + 2) * two : (o + 3) * two] = product(
                x_rows[:, (low + 1) * two : (high + 2) * two],
                panel(p_win, P_HALO, i, o, low, high),
            )

    wait_halo(1)

    @pl.loop(0, rows // 2)
    def _(i):
        for o in range(-3, 4):
            low, high = max(-2, o - 1), min(2, o + 1)
            weighted[:, (o + 3) * two : (o + 4) * two] = product(
                factors[i, pl.ds(0, two), (low + 2) * two : (high + 3) * two],
                panel(h_win, H_HALO, i, o, low, high),
            )
        for o in range(-2, 3):
            factors[i, pl.ds(two, two), (o + 2) * two : (o + 3) * two] = product(
                weighted[:, (o + 2) * two : (o + 5) * two],
                panel(p_win, P_HALO, i, o, o - 1, o + 1),
            )

    wait_halo(2)

    @pl.loop(0, rows // 2)
    def _(i):
        for o in range(-1, 2):
            both = product(
                factors[i, :, (o + 1) * two : (o + 4) * two],
                panel(x_win, X_HALO, i, o, o - 1, o + 1),
            )
            store(d_out, i, o, both[:two])
            store(e_out, i, o, both[two:])

    d_copy = pltpu.make_async_copy(d_out, d_hbm, out_sem.at[0])
    d_copy.start()
    e_copy = pltpu.make_async_copy(e_out, e_hbm, out_sem.at[1])
    e_copy.start()

    @pl.loop(1, group)
    def _(rel):
        meta_copy(rel).wait_send()
        p_copy(rel).wait_send()
        h_copy(rel, 0).wait_send()
        h_copy(rel, 1).wait_send()

    for m in range(3):
        wait_halo_sent(m)
    d_copy.wait()
    e_copy.wait()


def solution(mesh):
    domains, group = mesh.shape["grid"], mesh.shape["dom"]
    side = 4

    def shards(home, p_grid, p_mask, h_grid, h_mask, x_inv, x_mask):
        rows, band, block, _ = p_grid.shape
        kind = p_grid.dtype
        two = 2 * block
        own = (rows, band, block, block)
        slots = (group, band, block, block)
        out = jax.ShapeDtypeStruct(own, kind)
        anywhere = pl.BlockSpec(memory_space=pl.ANY)
        return pl.pallas_call(
            functools.partial(kernel, domains, group, side, rows),
            out_shape=(out, out),
            in_specs=[anywhere] * 7,
            out_specs=(anywhere, anywhere),
            scratch_shapes=[
                pltpu.VMEM(own, kind),
                pltpu.VMEM(own, kind),
                pltpu.VMEM(own, kind),
                pltpu.VMEM(slots, kind),
                pltpu.VMEM(slots, kind),
                pltpu.VMEM(slots, kind),
                pltpu.VMEM((group, H_CUTS[0][1], block, block), kind),
                pltpu.VMEM((group, H_CUTS[1][1], block, block), kind),
                pltpu.VMEM((rows + 2 * P_HALO, band, block, block), kind),
                pltpu.VMEM((rows + 2 * H_HALO, band, block, block), kind),
                pltpu.VMEM((rows + 2 * X_HALO, band, block, block), kind),
                pltpu.VMEM((rows // 2, 2 * two, 5 * two), kind),
                pltpu.VMEM((two, 7 * two), kind),
                pltpu.VMEM(own, kind),
                pltpu.VMEM(own, kind),
                pltpu.VMEM((8, 128), jnp.int32),
                pltpu.VMEM((group, 8, 128), jnp.int32),
                pltpu.SMEM((group, 1, 128), jnp.int32),
                pltpu.SMEM((rows,), jnp.int32),
                pltpu.SMEM((rows, band), jnp.int32),
                pltpu.SMEM((rows, band), jnp.int32),
                pltpu.SMEM((rows, band), jnp.int32),
                pltpu.SemaphoreType.DMA((8,)),
                pltpu.SemaphoreType.DMA((4, group)),
                pltpu.SemaphoreType.DMA((4, group)),
                pltpu.SemaphoreType.DMA((3, 2, 5)),
                pltpu.SemaphoreType.DMA((3, 2, 5)),
                pltpu.SemaphoreType.DMA((2,)),
            ],
            compiler_params=pltpu.CompilerParams(
                collective_id=0, has_side_effects=True, vmem_limit_bytes=60 << 20
            ),
        )(home, p_mask, h_mask, x_mask, p_grid, h_grid, x_inv)

    rows_spec = P(("grid", "dom"))
    return jax.shard_map(
        shards,
        mesh=mesh,
        in_specs=(rows_spec,) * 7,
        out_specs=(rows_spec, rows_spec),
        check_vma=False,
    )
```

```python
import functools

import jax
import jax.numpy as jnp
from jax import lax
from jax.experimental import pallas as pl
from jax.experimental.pallas import tpu as pltpu
from jax.sharding import PartitionSpec as P

MESH = pl.DeviceIdType.MESH
BAND = 5
P_HALO, H_HALO, X_HALO = 6, 4, 4

P_PARTS = ((2, 2, 0, 5), (3, 1, 1, 4), (4, 1, 2, 3), (5, 1, 3, 2), (6, 1, 4, 1))
H_CUTS = ((0, 3), (3, 2))
H_PARTS = tuple((4, 4, b0, nb) for b0, nb in H_CUTS)
X_PARTS = ((1, 1, 1, 4), (2, 1, 2, 3), (3, 1, 3, 2), (4, 1, 4, 1))
ORDER = (
    (1, 0), (0, 1), (3, 0), (0, 3), (2, 0), (0, 2), (1, 1), (3, 3),
    (1, 3), (3, 1), (2, 1), (2, 3), (1, 2), (3, 2), (2, 2),
)
PARTS = (P_PARTS, H_PARTS, X_PARTS)
HALOS = (P_HALO, H_HALO, X_HALO)


def kernel(
    domains,
    group,
    side,
    rows,
    home_hbm,
    p_mask_hbm,
    h_mask_hbm,
    x_mask_hbm,
    p_hbm,
    h_hbm,
    x_hbm,
    d_out,
    e_out,
    p_in,
    h_in,
    x_in,
    p_send,
    h_send,
    p_recv,
    h_recv_0,
    h_recv_1,
    p_win,
    h_win,
    x_win,
    factors,
    weighted,
    meta_send,
    meta_recv,
    meta,
    home,
    p_mask,
    h_mask,
    x_mask,
    local_sem,
    slot_send,
    slot_recv,
    halo_send,
    halo_recv,
):
    g, t = lax.axis_index("grid"), lax.axis_index("dom")
    tx, tz = t // side, t % side
    block = p_in.shape[-1]
    me = g * group + t
    has_next, has_prev = me < domains * group - 1, me > 0
    after = lax.rem(me + 1, domains * group)
    before = lax.rem(me + domains * group - 1, domains * group)
    next_id = (after // group, after % group)
    prev_id = (before // group, before % group)

    def target(rel):
        return lax.rem(tx + rel // side, side) * side + lax.rem(tz + rel % side, side)

    loads = [
        pltpu.make_async_copy(src, dst, local_sem.at[i])
        for i, (src, dst) in enumerate(
            (
                (home_hbm, home),
                (p_mask_hbm, p_mask),
                (p_hbm, p_in),
                (x_mask_hbm, x_mask),
                (x_hbm, x_in),
                (h_mask_hbm, h_mask),
                (h_hbm, h_in),
            )
        )
    ]
    for load in loads:
        load.start()

    barrier = pltpu.get_barrier_semaphore()

    @pl.loop(1, group)
    def _(rel):
        pl.semaphore_signal(barrier, inc=1, device_id=(g, target(rel)), device_id_type=MESH)

    cross_next = (t == group - 1) & has_next
    cross_prev = (t == 0) & has_prev

    @pl.when(cross_next)
    def _():
        pl.semaphore_signal(barrier, inc=1, device_id=next_id, device_id_type=MESH)

    @pl.when(cross_prev)
    def _():
        pl.semaphore_signal(barrier, inc=1, device_id=prev_id, device_id_type=MESH)

    loads[0].wait()
    homes = [home[r] for r in range(rows)]
    devs = [(h // rows) % group for h in homes]
    lane = lax.broadcasted_iota(jnp.int32, (8, 128), 1)
    packed = jnp.zeros((8, 128), jnp.int32)
    for r in range(rows):
        packed = jnp.where(lane == r, homes[r], packed)
    meta_send[...] = packed
    meta_recv[0] = packed

    def slot_copy(kind, src, dst, rel):
        return pltpu.make_async_remote_copy(
            src_ref=src,
            dst_ref=dst,
            send_sem=slot_send.at[kind, rel],
            recv_sem=slot_recv.at[kind, rel],
            device_id=(g, target(rel)),
            device_id_type=MESH,
        )

    def meta_copy(rel):
        return slot_copy(2, meta_send, meta_recv.at[rel], rel)

    def p_copy(rel):
        return slot_copy(0, p_send.at[rel], p_recv.at[rel], rel)

    h_recv = (h_recv_0, h_recv_1)

    def h_copy(rel, part):
        cut = pl.ds(*H_CUTS[part])
        return slot_copy((1, 3)[part], h_send.at[rel, cut], h_recv[part].at[rel], rel)

    def masked(ref, mask, row, b):
        scale = jnp.full((block, block), mask[row, b].astype(jnp.float32)).astype(jnp.bfloat16)
        return ref[row, b] * scale

    def fill(ref, mask, out, slot, rel, first=0, count=BAND):
        to = target(rel)
        row = jnp.int32(0)
        for r in range(rows):
            row = jnp.where(devs[r] == to, r, row)
        for b in range(count):
            out[slot, b] = masked(ref, mask, row, first + b)

    order = [dx * side + dz for dx, dz in ORDER]
    loads[1].wait()
    loads[2].wait()
    for rel in order:
        fill(p_in, p_mask, p_send, rel, rel)

    cross = cross_next.astype(jnp.int32) + cross_prev.astype(jnp.int32)
    pl.semaphore_wait(barrier, group - 1 + cross)

    @pl.loop(1, group)
    def _(rel):
        meta_copy(rel).start()

    for rel in order:
        p_copy(rel).start()

    fill(p_in, p_mask, p_recv, 0, 0)

    windows = (p_win, h_win, x_win)

    def halo_copies(m):
        win, halo = windows[m], HALOS[m]
        up, down = [], []
        for c, (far, n, b0, nb) in enumerate(PARTS[m]):
            low = halo + rows - far
            up.append(
                pltpu.make_async_remote_copy(
                    src_ref=win.at[pl.ds(low, n), pl.ds(b0, nb)],
                    dst_ref=win.at[pl.ds(low - rows, n), pl.ds(b0, nb)],
                    send_sem=halo_send.at[m, 0, c],
                    recv_sem=halo_recv.at[m, 0, c],
                    device_id=next_id,
                    device_id_type=MESH,
                )
            )
            high, b1 = halo + far - n, b0 if m == 1 else BAND - b0 - nb
            down.append(
                pltpu.make_async_remote_copy(
                    src_ref=win.at[pl.ds(high, n), pl.ds(b1, nb)],
                    dst_ref=win.at[pl.ds(high + rows, n), pl.ds(b1, nb)],
                    send_sem=halo_send.at[m, 1, c],
                    recv_sem=halo_recv.at[m, 1, c],
                    device_id=prev_id,
                    device_id_type=MESH,
                )
            )
        return up, down

    def start_halo(m, parts=None):
        up, down = halo_copies(m)
        for c in range(len(up)) if parts is None else parts:
            pl.when(has_next)(up[c].start)
            pl.when(has_prev)(down[c].start)

    def wait_halo(m):
        up, down = halo_copies(m)

        @pl.when(has_prev)
        def _():
            for copy in up:
                copy.wait_recv()

        @pl.when(has_next)
        def _():
            for copy in down:
                copy.wait_recv()

    def wait_halo_sent(m):
        up, down = halo_copies(m)

        @pl.when(has_next)
        def _():
            for copy in up:
                copy.wait_send()

        @pl.when(has_prev)
        def _():
            for copy in down:
                copy.wait_send()

    def clear(win, first, count):
        @pl.loop(first, first + count)
        def _(row):
            for b in range(BAND):
                win[row, b] = jnp.zeros((block, block), jnp.bfloat16)

    loads[3].wait()
    loads[4].wait()

    @pl.loop(0, rows)
    def _(row):
        for b in range(BAND):
            x_win[X_HALO + row, b] = masked(x_in, x_mask, row, b)

    loads[5].wait()
    loads[6].wait()
    for rel in order:
        fill(h_in, h_mask, h_send, rel, rel)
        h_copy(rel, 0).start()
    for rel in order:
        h_copy(rel, 1).start()

    for recv, cut in zip(h_recv, H_CUTS):
        fill(h_in, h_mask, recv, 0, 0, *cut)

    @pl.when(jnp.logical_not(has_prev))
    def _():
        for win, halo in zip(windows, HALOS):
            clear(win, 0, halo)

    @pl.when(jnp.logical_not(has_next))
    def _():
        for win, halo in zip(windows, HALOS):
            clear(win, halo + rows, halo)

    @pl.loop(1, group)
    def _(rel):
        meta_copy(rel).wait_recv()

    to_scalar = pltpu.make_async_copy(meta_recv.at[:, pl.ds(0, 1)], meta, local_sem.at[7])
    to_scalar.start()
    to_scalar.wait()

    def find(slot, found):
        for r in range(rows):
            value = meta[slot, 0, r]
            found = tuple(
                jnp.where(value == me * rows + j, slot, found[j]) for j in range(rows)
            )
        return found

    slots = lax.fori_loop(0, group, find, tuple(jnp.int32(0) for _ in range(rows)))

    def place(recv, win, halo, first=0, count=BAND):
        for j in range(rows):
            for b in range(count):
                win[halo + j, first + b] = recv[slots[j], b]

    @pl.loop(1, group)
    def _(rel):
        p_copy(rel).wait_recv()

    place(p_recv, p_win, P_HALO)
    start_halo(0)

    def piece(ref, halo, i, dr, dc):
        b = dc - dr + BAND // 2
        if 0 <= b < BAND:
            return ref[halo + 2 * i + dr, b]
        return jnp.zeros((block, block), jnp.bfloat16)

    def panel(ref, halo, i, o, low, high):
        return jnp.concatenate(
            [
                jnp.concatenate([piece(ref, halo, i, dr, 2 * o + c) for c in range(2)], 1)
                for dr in range(2 * low, 2 * high + 2)
            ],
            0,
        )

    def product(a, b):
        return jnp.dot(a, b, preferred_element_type=jnp.float32).astype(jnp.bfloat16)

    two = 2 * block

    def store(out, i, o, value):
        for r in range(2):
            for c in range(2):
                b = 2 * o + c - r + BAND // 2
                if 0 <= b < BAND:
                    out[2 * i + r, b] = value[
                        r * block : (r + 1) * block, c * block : (c + 1) * block
                    ]

    for part, cut in enumerate(H_CUTS):

        @pl.loop(1, group)
        def _(rel):
            h_copy(rel, part).wait_recv()

        place(h_recv[part], h_win, H_HALO, *cut)
        start_halo(1, (part,))

    start_halo(2)
    wait_halo(0)

    @pl.loop(0, rows // 2)
    def _(i):
        x_rows = jnp.concatenate(
            [
                jnp.concatenate([piece(x_win, X_HALO, i, r, dc) for dc in range(-2, 4)], 1)
                for r in range(2)
            ],
            0,
        )
        for o in range(-2, 3):
            low, high = max(-1, o - 1), min(1, o + 1)
            factors[i, pl.ds(0, two), (o + 2) * two : (o + 3) * two] = product(
                x_rows[:, (low + 1) * two : (high + 2) * two],
                panel(p_win, P_HALO, i, o, low, high),
            )

    wait_halo(1)

    @pl.loop(0, rows // 2)
    def _(i):
        for o in range(-3, 4):
            low, high = max(-2, o - 1), min(2, o + 1)
            weighted[:, (o + 3) * two : (o + 4) * two] = product(
                factors[i, pl.ds(0, two), (low + 2) * two : (high + 3) * two],
                panel(h_win, H_HALO, i, o, low, high),
            )
        for o in range(-2, 3):
            factors[i, pl.ds(two, two), (o + 2) * two : (o + 3) * two] = product(
                weighted[:, (o + 2) * two : (o + 5) * two],
                panel(p_win, P_HALO, i, o, o - 1, o + 1),
            )

    def with_x(i, o):
        both = product(
            factors[i, :, (o + 1) * two : (o + 4) * two],
            panel(x_win, X_HALO, i, o, o - 1, o + 1),
        )
        store(d_out, i, o, both[:two])
        store(e_out, i, o, both[two:])

    pairs = [(i, o) for i in range(rows // 2) for o in range(-1, 2)]
    inner = [(i, o) for i, o in pairs if 0 < i + o < rows // 2 - 1]
    for i, o in inner:
        with_x(i, o)
    wait_halo(2)
    for i, o in pairs:
        if (i, o) not in inner:
            with_x(i, o)


    @pl.loop(1, group)
    def _(rel):
        meta_copy(rel).wait_send()
        p_copy(rel).wait_send()
        h_copy(rel, 0).wait_send()
        h_copy(rel, 1).wait_send()

    for m in range(3):
        wait_halo_sent(m)


def solution(mesh):
    domains, group = mesh.shape["grid"], mesh.shape["dom"]
    side = 4

    def shards(home, p_grid, p_mask, h_grid, h_mask, x_inv, x_mask):
        rows, band, block, _ = p_grid.shape
        kind = p_grid.dtype
        two = 2 * block
        own = (rows, band, block, block)
        slots = (group, band, block, block)
        out = jax.ShapeDtypeStruct(own, kind)
        anywhere = pl.BlockSpec(memory_space=pl.ANY)
        return pl.pallas_call(
            functools.partial(kernel, domains, group, side, rows),
            out_shape=(out, out),
            in_specs=[anywhere] * 7,
            out_specs=(pl.BlockSpec(memory_space=pltpu.VMEM),) * 2,
            scratch_shapes=[
                pltpu.VMEM(own, kind),
                pltpu.VMEM(own, kind),
                pltpu.VMEM(own, kind),
                pltpu.VMEM(slots, kind),
                pltpu.VMEM(slots, kind),
                pltpu.VMEM(slots, kind),
                pltpu.VMEM((group, H_CUTS[0][1], block, block), kind),
                pltpu.VMEM((group, H_CUTS[1][1], block, block), kind),
                pltpu.VMEM((rows + 2 * P_HALO, band, block, block), kind),
                pltpu.VMEM((rows + 2 * H_HALO, band, block, block), kind),
                pltpu.VMEM((rows + 2 * X_HALO, band, block, block), kind),
                pltpu.VMEM((rows // 2, 2 * two, 5 * two), kind),
                pltpu.VMEM((two, 7 * two), kind),
                pltpu.VMEM((8, 128), jnp.int32),
                pltpu.VMEM((group, 8, 128), jnp.int32),
                pltpu.SMEM((group, 1, 128), jnp.int32),
                pltpu.SMEM((rows,), jnp.int32),
                pltpu.SMEM((rows, band), jnp.int32),
                pltpu.SMEM((rows, band), jnp.int32),
                pltpu.SMEM((rows, band), jnp.int32),
                pltpu.SemaphoreType.DMA((8,)),
                pltpu.SemaphoreType.DMA((4, group)),
                pltpu.SemaphoreType.DMA((4, group)),
                pltpu.SemaphoreType.DMA((3, 2, 5)),
                pltpu.SemaphoreType.DMA((3, 2, 5)),
            ],
            compiler_params=pltpu.CompilerParams(
                collective_id=0, has_side_effects=True, vmem_limit_bytes=51 << 20
            ),
        )(*(pltpu.with_memory_space_constraint(a, pltpu.HBM) for a in (home, p_mask, h_mask, x_mask, p_grid, h_grid, x_inv)))

    rows_spec = P(("grid", "dom"))
    return jax.shard_map(
        shards,
        mesh=mesh,
        in_specs=(rows_spec,) * 7,
        out_specs=(rows_spec, rows_spec),
        check_vma=False,
    )
```

```python
import functools

import jax
import jax.numpy as jnp
from jax import lax
from jax.experimental import pallas as pl
from jax.experimental.pallas import tpu as pltpu
from jax.sharding import PartitionSpec as P

MESH = pl.DeviceIdType.MESH
BAND = 5
P_HALO, H_HALO, X_HALO = 6, 4, 4

P_PARTS = ((2, 2, 0, 5), (3, 1, 1, 4), (4, 1, 2, 3), (5, 1, 3, 2), (6, 1, 4, 1))
H_CUTS = ((0, 5),)
H_PARTS = tuple((4, 4, b0, nb) for b0, nb in H_CUTS)
X_PARTS = ((1, 1, 1, 4), (2, 1, 2, 3), (3, 1, 3, 2), (4, 1, 4, 1))
ORDER = (
    (2, 2), (1, 2), (3, 0), (2, 1), (0, 3), (1, 1), (3, 3), (2, 0),
    (0, 2), (3, 2), (1, 0), (2, 3), (0, 1), (1, 3), (3, 1),
)
PARTS = (P_PARTS, H_PARTS, X_PARTS)
HALOS = (P_HALO, H_HALO, X_HALO)


def kernel(
    domains,
    group,
    side,
    rows,
    home_hbm,
    p_mask_hbm,
    h_mask_hbm,
    x_mask_hbm,
    p_hbm,
    h_hbm,
    x_hbm,
    d_out,
    e_out,
    p_in,
    h_in,
    x_in,
    p_send,
    h_send,
    p_recv,
    h_recv_0,
    p_win,
    h_win,
    x_win,
    factors,
    weighted,
    meta_send,
    meta_recv,
    meta,
    home,
    p_mask,
    h_mask,
    x_mask,
    local_sem,
    slot_send,
    slot_recv,
    halo_send,
    halo_recv,
):
    g, t = lax.axis_index("grid"), lax.axis_index("dom")
    tx, tz = t // side, t % side
    block = p_in.shape[-1]
    me = g * group + t
    has_next, has_prev = me < domains * group - 1, me > 0
    after = lax.rem(me + 1, domains * group)
    before = lax.rem(me + domains * group - 1, domains * group)
    next_id = (after // group, after % group)
    prev_id = (before // group, before % group)

    def target(rel):
        return lax.rem(tx + rel // side, side) * side + lax.rem(tz + rel % side, side)

    loads = [
        pltpu.make_async_copy(src, dst, local_sem.at[i])
        for i, (src, dst) in enumerate(
            (
                (home_hbm, home),
                (p_mask_hbm, p_mask),
                (p_hbm, p_in),
                (x_mask_hbm, x_mask),
                (x_hbm, x_in),
                (h_mask_hbm, h_mask),
                (h_hbm, h_in),
            )
        )
    ]
    for load in loads:
        load.start()

    barrier = pltpu.get_barrier_semaphore()

    for dx, dz in ORDER:
        pl.semaphore_signal(
            barrier, inc=1, device_id=(g, target(dx * side + dz)), device_id_type=MESH
        )

    cross_next = (t == group - 1) & has_next
    cross_prev = (t == 0) & has_prev

    @pl.when(cross_next)
    def _():
        pl.semaphore_signal(barrier, inc=1, device_id=next_id, device_id_type=MESH)

    @pl.when(cross_prev)
    def _():
        pl.semaphore_signal(barrier, inc=1, device_id=prev_id, device_id_type=MESH)

    loads[0].wait()
    homes = [home[r] for r in range(rows)]
    devs = [(h // rows) % group for h in homes]
    lane = lax.broadcasted_iota(jnp.int32, (8, 128), 1)
    packed = jnp.zeros((8, 128), jnp.int32)
    for r in range(rows):
        packed = jnp.where(lane == r, homes[r], packed)
    meta_send[...] = packed
    meta_recv[0] = packed

    def slot_copy(kind, src, dst, rel):
        return pltpu.make_async_remote_copy(
            src_ref=src,
            dst_ref=dst,
            send_sem=slot_send.at[kind, rel],
            recv_sem=slot_recv.at[kind, rel],
            device_id=(g, target(rel)),
            device_id_type=MESH,
        )

    def meta_copy(rel):
        return slot_copy(2, meta_send, meta_recv.at[rel], rel)

    def p_copy(rel):
        return slot_copy(0, p_send.at[rel], p_recv.at[rel], rel)

    h_recv = (h_recv_0,)

    def h_copy(rel, part):
        cut = pl.ds(*H_CUTS[part])
        return slot_copy((1, 3)[part], h_send.at[rel, cut], h_recv[part].at[rel], rel)

    def masked(ref, mask, row, b):
        scale = jnp.full((block, block), mask[row, b].astype(jnp.float32)).astype(jnp.bfloat16)
        return ref[row, b] * scale

    def fill(ref, mask, out, slot, rel, first=0, count=BAND):
        to = target(rel)
        row = jnp.int32(0)
        for r in range(rows):
            row = jnp.where(devs[r] == to, r, row)
        for b in range(count):
            out[slot, b] = masked(ref, mask, row, first + b)

    order = [dx * side + dz for dx, dz in ORDER]
    loads[1].wait()
    loads[2].wait()
    for rel in order:
        fill(p_in, p_mask, p_send, rel, rel)

    cross = cross_next.astype(jnp.int32) + cross_prev.astype(jnp.int32)
    pl.semaphore_wait(barrier, group - 1 + cross)

    @pl.loop(1, group)
    def _(rel):
        meta_copy(rel).start()

    for rel in order:
        p_copy(rel).start()

    fill(p_in, p_mask, p_recv, 0, 0)

    windows = (p_win, h_win, x_win)

    def halo_copies(m):
        win, halo = windows[m], HALOS[m]
        up, down = [], []
        for c, (far, n, b0, nb) in enumerate(PARTS[m]):
            low = halo + rows - far
            up.append(
                pltpu.make_async_remote_copy(
                    src_ref=win.at[pl.ds(low, n), pl.ds(b0, nb)],
                    dst_ref=win.at[pl.ds(low - rows, n), pl.ds(b0, nb)],
                    send_sem=halo_send.at[m, 0, c],
                    recv_sem=halo_recv.at[m, 0, c],
                    device_id=next_id,
                    device_id_type=MESH,
                )
            )
            high, b1 = halo + far - n, b0 if m == 1 else BAND - b0 - nb
            down.append(
                pltpu.make_async_remote_copy(
                    src_ref=win.at[pl.ds(high, n), pl.ds(b1, nb)],
                    dst_ref=win.at[pl.ds(high + rows, n), pl.ds(b1, nb)],
                    send_sem=halo_send.at[m, 1, c],
                    recv_sem=halo_recv.at[m, 1, c],
                    device_id=prev_id,
                    device_id_type=MESH,
                )
            )
        return up, down

    def start_halo(m, parts=None):
        up, down = halo_copies(m)
        for c in range(len(up)) if parts is None else parts:
            pl.when(has_next)(up[c].start)
            pl.when(has_prev)(down[c].start)

    def wait_halo(m):
        up, down = halo_copies(m)

        @pl.when(has_prev)
        def _():
            for copy in up:
                copy.wait_recv()

        @pl.when(has_next)
        def _():
            for copy in down:
                copy.wait_recv()

    def wait_halo_sent(m):
        up, down = halo_copies(m)

        @pl.when(has_next)
        def _():
            for copy in up:
                copy.wait_send()

        @pl.when(has_prev)
        def _():
            for copy in down:
                copy.wait_send()

    def clear(win, first, count):
        @pl.loop(first, first + count)
        def _(row):
            for b in range(BAND):
                win[row, b] = jnp.zeros((block, block), jnp.bfloat16)

    loads[3].wait()
    loads[4].wait()

    @pl.loop(0, rows)
    def _(row):
        for b in range(BAND):
            x_win[X_HALO + row, b] = masked(x_in, x_mask, row, b)

    loads[5].wait()
    loads[6].wait()
    for rel in order:
        fill(h_in, h_mask, h_send, rel, rel)
        h_copy(rel, 0).start()

    for recv, cut in zip(h_recv, H_CUTS):
        fill(h_in, h_mask, recv, 0, 0, *cut)

    @pl.when(jnp.logical_not(has_prev))
    def _():
        for win, halo in zip(windows, HALOS):
            clear(win, 0, halo)

    @pl.when(jnp.logical_not(has_next))
    def _():
        for win, halo in zip(windows, HALOS):
            clear(win, halo + rows, halo)

    @pl.loop(1, group)
    def _(rel):
        meta_copy(rel).wait_recv()

    to_scalar = pltpu.make_async_copy(meta_recv.at[:, pl.ds(0, 1)], meta, local_sem.at[7])
    to_scalar.start()
    to_scalar.wait()

    def find(slot, found):
        for r in range(rows):
            value = meta[slot, 0, r]
            found = tuple(
                jnp.where(value == me * rows + j, slot, found[j]) for j in range(rows)
            )
        return found

    slots = lax.fori_loop(0, group, find, tuple(jnp.int32(0) for _ in range(rows)))

    def place(recv, win, halo, first=0, count=BAND):
        for j in range(rows):
            for b in range(count):
                win[halo + j, first + b] = recv[slots[j], b]

    @pl.loop(1, group)
    def _(rel):
        p_copy(rel).wait_recv()

    place(p_recv, p_win, P_HALO)
    start_halo(0)

    def piece(ref, halo, i, dr, dc):
        b = dc - dr + BAND // 2
        if 0 <= b < BAND:
            return ref[halo + 2 * i + dr, b]
        return jnp.zeros((block, block), jnp.bfloat16)

    def panel(ref, halo, i, o, low, high):
        return jnp.concatenate(
            [
                jnp.concatenate([piece(ref, halo, i, dr, 2 * o + c) for c in range(2)], 1)
                for dr in range(2 * low, 2 * high + 2)
            ],
            0,
        )

    def product(a, b):
        return jnp.dot(a, b, preferred_element_type=jnp.float32).astype(jnp.bfloat16)

    two = 2 * block

    def store(out, i, o, value):
        for r in range(2):
            for c in range(2):
                b = 2 * o + c - r + BAND // 2
                if 0 <= b < BAND:
                    out[2 * i + r, b] = value[
                        r * block : (r + 1) * block, c * block : (c + 1) * block
                    ]

    for part, cut in enumerate(H_CUTS):

        @pl.loop(1, group)
        def _(rel):
            h_copy(rel, part).wait_recv()

        place(h_recv[part], h_win, H_HALO, *cut)
        start_halo(1, (part,))

    start_halo(2)
    wait_halo(0)

    @pl.loop(0, rows // 2)
    def _(i):
        x_rows = jnp.concatenate(
            [
                jnp.concatenate([piece(x_win, X_HALO, i, r, dc) for dc in range(-2, 4)], 1)
                for r in range(2)
            ],
            0,
        )
        for o in range(-2, 3):
            low, high = max(-1, o - 1), min(1, o + 1)
            factors[i, pl.ds(0, two), (o + 2) * two : (o + 3) * two] = product(
                x_rows[:, (low + 1) * two : (high + 2) * two],
                panel(p_win, P_HALO, i, o, low, high),
            )

    wait_halo(1)

    @pl.loop(0, rows // 2)
    def _(i):
        for o in range(-3, 4):
            low, high = max(-2, o - 1), min(2, o + 1)
            weighted[:, (o + 3) * two : (o + 4) * two] = product(
                factors[i, pl.ds(0, two), (low + 2) * two : (high + 3) * two],
                panel(h_win, H_HALO, i, o, low, high),
            )
        for o in range(-2, 3):
            factors[i, pl.ds(two, two), (o + 2) * two : (o + 3) * two] = product(
                weighted[:, (o + 2) * two : (o + 5) * two],
                panel(p_win, P_HALO, i, o, o - 1, o + 1),
            )

    def with_x(i, o):
        both = product(
            factors[i, :, (o + 1) * two : (o + 4) * two],
            panel(x_win, X_HALO, i, o, o - 1, o + 1),
        )
        store(d_out, i, o, both[:two])
        store(e_out, i, o, both[two:])

    pairs = [(i, o) for i in range(rows // 2) for o in range(-1, 2)]
    inner = [(i, o) for i, o in pairs if 0 < i + o < rows // 2 - 1]
    for i, o in inner:
        with_x(i, o)
    wait_halo(2)
    for i, o in pairs:
        if (i, o) not in inner:
            with_x(i, o)


    @pl.loop(1, group)
    def _(rel):
        meta_copy(rel).wait_send()
        p_copy(rel).wait_send()
        h_copy(rel, 0).wait_send()

    for m in range(3):
        wait_halo_sent(m)


def solution(mesh):
    domains, group = mesh.shape["grid"], mesh.shape["dom"]
    side = 4

    def shards(home, p_grid, p_mask, h_grid, h_mask, x_inv, x_mask):
        rows, band, block, _ = p_grid.shape
        kind = p_grid.dtype
        two = 2 * block
        own = (rows, band, block, block)
        slots = (group, band, block, block)
        out = jax.ShapeDtypeStruct(own, kind)
        anywhere = pl.BlockSpec(memory_space=pl.ANY)
        return pl.pallas_call(
            functools.partial(kernel, domains, group, side, rows),
            out_shape=(out, out),
            in_specs=[anywhere] * 7,
            out_specs=(pl.BlockSpec(memory_space=pltpu.VMEM),) * 2,
            scratch_shapes=[
                pltpu.VMEM(own, kind),
                pltpu.VMEM(own, kind),
                pltpu.VMEM(own, kind),
                pltpu.VMEM(slots, kind),
                pltpu.VMEM(slots, kind),
                pltpu.VMEM(slots, kind),
                pltpu.VMEM((group, H_CUTS[0][1], block, block), kind),
                pltpu.VMEM((rows + 2 * P_HALO, band, block, block), kind),
                pltpu.VMEM((rows + 2 * H_HALO, band, block, block), kind),
                pltpu.VMEM((rows + 2 * X_HALO, band, block, block), kind),
                pltpu.VMEM((rows // 2, 2 * two, 5 * two), kind),
                pltpu.VMEM((two, 7 * two), kind),
                pltpu.VMEM((8, 128), jnp.int32),
                pltpu.VMEM((group, 8, 128), jnp.int32),
                pltpu.SMEM((group, 1, 128), jnp.int32),
                pltpu.SMEM((rows,), jnp.int32),
                pltpu.SMEM((rows, band), jnp.int32),
                pltpu.SMEM((rows, band), jnp.int32),
                pltpu.SMEM((rows, band), jnp.int32),
                pltpu.SemaphoreType.DMA((8,)),
                pltpu.SemaphoreType.DMA((4, group)),
                pltpu.SemaphoreType.DMA((4, group)),
                pltpu.SemaphoreType.DMA((3, 2, 5)),
                pltpu.SemaphoreType.DMA((3, 2, 5)),
            ],
            compiler_params=pltpu.CompilerParams(
                collective_id=0, has_side_effects=True, vmem_limit_bytes=51 << 20
            ),
        )(*(pltpu.with_memory_space_constraint(a, pltpu.HBM) for a in (home, p_mask, h_mask, x_mask, p_grid, h_grid, x_inv)))

    rows_spec = P(("grid", "dom"))
    return jax.shard_map(
        shards,
        mesh=mesh,
        in_specs=(rows_spec,) * 7,
        out_specs=(rows_spec, rows_spec),
        check_vma=False,
    )
```

```python
import functools

import jax
import jax.numpy as jnp
from jax import lax
from jax.experimental import pallas as pl
from jax.experimental.pallas import tpu as pltpu
from jax.sharding import PartitionSpec as P

MESH = pl.DeviceIdType.MESH
BAND = 5
P_HALO, H_HALO, X_HALO = 6, 4, 4

P_PARTS = ((2, 2, 0, 5), (3, 1, 1, 4), (4, 1, 2, 3), (5, 1, 3, 2), (6, 1, 4, 1))
H_CUTS = ((0, 5),)
H_PARTS = tuple((4, 4, b0, nb) for b0, nb in H_CUTS)
X_PARTS = ((1, 1, 1, 4), (2, 1, 2, 3), (3, 1, 3, 2), (4, 1, 4, 1))
ORDER = ((2, 2), (1, 2), (3, 0), (2, 1), (0, 3), (3, 2), (1, 0), (2, 3), (0, 1), (2, 0), (0, 2), (1, 1), (3, 3), (1, 3), (3, 1),
)
PARTS = (P_PARTS, H_PARTS, X_PARTS)
HALOS = (P_HALO, H_HALO, X_HALO)


def kernel(
    domains,
    group,
    side,
    rows,
    home_hbm,
    p_mask_hbm,
    h_mask_hbm,
    x_mask_hbm,
    p_hbm,
    h_hbm,
    x_hbm,
    d_out,
    e_out,
    p_in,
    h_in,
    x_in,
    p_send,
    h_send,
    p_recv,
    h_recv_0,
    p_win,
    h_win,
    x_win,
    factors,
    weighted,
    meta_send,
    meta_recv,
    meta,
    home,
    p_mask,
    h_mask,
    x_mask,
    local_sem,
    slot_send,
    slot_recv,
    halo_send,
    halo_recv,
):
    g, t = lax.axis_index("grid"), lax.axis_index("dom")
    tx, tz = t // side, t % side
    block = p_in.shape[-1]
    me = g * group + t
    has_next, has_prev = me < domains * group - 1, me > 0
    after = lax.rem(me + 1, domains * group)
    before = lax.rem(me + domains * group - 1, domains * group)
    next_id = (after // group, after % group)
    prev_id = (before // group, before % group)

    def target(rel):
        return lax.rem(tx + rel // side, side) * side + lax.rem(tz + rel % side, side)

    loads = [
        pltpu.make_async_copy(src, dst, local_sem.at[i])
        for i, (src, dst) in enumerate(
            (
                (home_hbm, home),
                (p_mask_hbm, p_mask),
                (p_hbm, p_in),
                (x_mask_hbm, x_mask),
                (x_hbm, x_in),
                (h_mask_hbm, h_mask),
                (h_hbm, h_in),
            )
        )
    ]
    for load in loads:
        load.start()

    barrier = pltpu.get_barrier_semaphore()

    for dx, dz in ORDER:
        pl.semaphore_signal(
            barrier, inc=1, device_id=(g, target(dx * side + dz)), device_id_type=MESH
        )

    cross_next = (t == group - 1) & has_next
    cross_prev = (t == 0) & has_prev

    @pl.when(cross_next)
    def _():
        pl.semaphore_signal(barrier, inc=1, device_id=next_id, device_id_type=MESH)

    @pl.when(cross_prev)
    def _():
        pl.semaphore_signal(barrier, inc=1, device_id=prev_id, device_id_type=MESH)

    loads[0].wait()
    homes = [home[r] for r in range(rows)]
    devs = [(h // rows) % group for h in homes]
    lane = lax.broadcasted_iota(jnp.int32, (8, 128), 1)
    packed = jnp.zeros((8, 128), jnp.int32)
    for r in range(rows):
        packed = jnp.where(lane == r, homes[r], packed)
    meta_send[...] = packed
    meta_recv[0] = packed

    def slot_copy(kind, src, dst, rel):
        return pltpu.make_async_remote_copy(
            src_ref=src,
            dst_ref=dst,
            send_sem=slot_send.at[kind, rel],
            recv_sem=slot_recv.at[kind, rel],
            device_id=(g, target(rel)),
            device_id_type=MESH,
        )

    def meta_copy(rel):
        return slot_copy(2, meta_send, meta_recv.at[rel], rel)

    def p_copy(rel):
        return slot_copy(0, p_send.at[rel], p_recv.at[rel], rel)

    h_recv = (h_recv_0,)

    def h_copy(rel, part):
        cut = pl.ds(*H_CUTS[part])
        return slot_copy((1, 3)[part], h_send.at[rel, cut], h_recv[part].at[rel], rel)

    def masked(ref, mask, row, b):
        scale = jnp.full((block, block), mask[row, b].astype(jnp.float32)).astype(jnp.bfloat16)
        return ref[row, b] * scale

    def fill(ref, mask, out, slot, rel, first=0, count=BAND):
        to = target(rel)
        row = jnp.int32(0)
        for r in range(rows):
            row = jnp.where(devs[r] == to, r, row)
        for b in range(count):
            out[slot, b] = masked(ref, mask, row, first + b)

    order = [dx * side + dz for dx, dz in ORDER]
    loads[1].wait()
    loads[2].wait()
    for rel in order:
        fill(p_in, p_mask, p_send, rel, rel)

    cross = cross_next.astype(jnp.int32) + cross_prev.astype(jnp.int32)
    pl.semaphore_wait(barrier, group - 1 + cross)

    @pl.loop(1, group)
    def _(rel):
        meta_copy(rel).start()

    for rel in order:
        p_copy(rel).start()

    fill(p_in, p_mask, p_recv, 0, 0)

    windows = (p_win, h_win, x_win)

    def halo_copies(m):
        win, halo = windows[m], HALOS[m]
        up, down = [], []
        for c, (far, n, b0, nb) in enumerate(PARTS[m]):
            low = halo + rows - far
            up.append(
                pltpu.make_async_remote_copy(
                    src_ref=win.at[pl.ds(low, n), pl.ds(b0, nb)],
                    dst_ref=win.at[pl.ds(low - rows, n), pl.ds(b0, nb)],
                    send_sem=halo_send.at[m, 0, c],
                    recv_sem=halo_recv.at[m, 0, c],
                    device_id=next_id,
                    device_id_type=MESH,
                )
            )
            high, b1 = halo + far - n, b0 if m == 1 else BAND - b0 - nb
            down.append(
                pltpu.make_async_remote_copy(
                    src_ref=win.at[pl.ds(high, n), pl.ds(b1, nb)],
                    dst_ref=win.at[pl.ds(high + rows, n), pl.ds(b1, nb)],
                    send_sem=halo_send.at[m, 1, c],
                    recv_sem=halo_recv.at[m, 1, c],
                    device_id=prev_id,
                    device_id_type=MESH,
                )
            )
        return up, down

    def start_halo(m, parts=None):
        up, down = halo_copies(m)
        for c in range(len(up)) if parts is None else parts:
            pl.when(has_next)(up[c].start)
            pl.when(has_prev)(down[c].start)

    def wait_halo(m):
        up, down = halo_copies(m)

        @pl.when(has_prev)
        def _():
            for copy in up:
                copy.wait_recv()

        @pl.when(has_next)
        def _():
            for copy in down:
                copy.wait_recv()

    def wait_halo_sent(m):
        up, down = halo_copies(m)

        @pl.when(has_next)
        def _():
            for copy in up:
                copy.wait_send()

        @pl.when(has_prev)
        def _():
            for copy in down:
                copy.wait_send()

    def clear(win, first, count):
        @pl.loop(first, first + count)
        def _(row):
            for b in range(BAND):
                win[row, b] = jnp.zeros((block, block), jnp.bfloat16)

    loads[3].wait()
    loads[4].wait()

    @pl.loop(0, rows)
    def _(row):
        for b in range(BAND):
            x_win[X_HALO + row, b] = masked(x_in, x_mask, row, b)

    loads[5].wait()
    loads[6].wait()
    for rel in order:
        fill(h_in, h_mask, h_send, rel, rel)
        h_copy(rel, 0).start()

    for recv, cut in zip(h_recv, H_CUTS):
        fill(h_in, h_mask, recv, 0, 0, *cut)

    @pl.when(jnp.logical_not(has_prev))
    def _():
        for win, halo in zip(windows, HALOS):
            clear(win, 0, halo)

    @pl.when(jnp.logical_not(has_next))
    def _():
        for win, halo in zip(windows, HALOS):
            clear(win, halo + rows, halo)

    @pl.loop(1, group)
    def _(rel):
        meta_copy(rel).wait_recv()

    to_scalar = pltpu.make_async_copy(meta_recv.at[:, pl.ds(0, 1)], meta, local_sem.at[7])
    to_scalar.start()
    to_scalar.wait()

    def find(slot, found):
        for r in range(rows):
            value = meta[slot, 0, r]
            found = tuple(
                jnp.where(value == me * rows + j, slot, found[j]) for j in range(rows)
            )
        return found

    slots = lax.fori_loop(0, group, find, tuple(jnp.int32(0) for _ in range(rows)))

    def place(recv, win, halo, first=0, count=BAND):
        for j in range(rows):
            for b in range(count):
                win[halo + j, first + b] = recv[slots[j], b]

    @pl.loop(1, group)
    def _(rel):
        p_copy(rel).wait_recv()

    place(p_recv, p_win, P_HALO)
    start_halo(0)

    def piece(ref, halo, i, dr, dc):
        b = dc - dr + BAND // 2
        if 0 <= b < BAND:
            return ref[halo + 2 * i + dr, b]
        return jnp.zeros((block, block), jnp.bfloat16)

    def panel(ref, halo, i, o, low, high):
        return jnp.concatenate(
            [
                jnp.concatenate([piece(ref, halo, i, dr, 2 * o + c) for c in range(2)], 1)
                for dr in range(2 * low, 2 * high + 2)
            ],
            0,
        )

    def product(a, b):
        return jnp.dot(a, b, preferred_element_type=jnp.float32).astype(jnp.bfloat16)

    two = 2 * block

    def store(out, i, o, value):
        for r in range(2):
            for c in range(2):
                b = 2 * o + c - r + BAND // 2
                if 0 <= b < BAND:
                    out[2 * i + r, b] = value[
                        r * block : (r + 1) * block, c * block : (c + 1) * block
                    ]

    for part, cut in enumerate(H_CUTS):

        @pl.loop(1, group)
        def _(rel):
            h_copy(rel, part).wait_recv()

        place(h_recv[part], h_win, H_HALO, *cut)
        start_halo(1, (part,))

    start_halo(2)
    wait_halo(0)

    @pl.loop(0, rows // 2)
    def _(i):
        x_rows = jnp.concatenate(
            [
                jnp.concatenate([piece(x_win, X_HALO, i, r, dc) for dc in range(-2, 4)], 1)
                for r in range(2)
            ],
            0,
        )
        for o in range(-2, 3):
            low, high = max(-1, o - 1), min(1, o + 1)
            factors[i, pl.ds(0, two), (o + 2) * two : (o + 3) * two] = product(
                x_rows[:, (low + 1) * two : (high + 2) * two],
                panel(p_win, P_HALO, i, o, low, high),
            )

    wait_halo(1)

    @pl.loop(0, rows // 2)
    def _(i):
        for o in range(-3, 4):
            low, high = max(-2, o - 1), min(2, o + 1)
            weighted[:, (o + 3) * two : (o + 4) * two] = product(
                factors[i, pl.ds(0, two), (low + 2) * two : (high + 3) * two],
                panel(h_win, H_HALO, i, o, low, high),
            )
        for o in range(-2, 3):
            factors[i, pl.ds(two, two), (o + 2) * two : (o + 3) * two] = product(
                weighted[:, (o + 2) * two : (o + 5) * two],
                panel(p_win, P_HALO, i, o, o - 1, o + 1),
            )

    def with_x(i, o):
        both = product(
            factors[i, :, (o + 1) * two : (o + 4) * two],
            panel(x_win, X_HALO, i, o, o - 1, o + 1),
        )
        store(d_out, i, o, both[:two])
        store(e_out, i, o, both[two:])

    pairs = [(i, o) for i in range(rows // 2) for o in range(-1, 2)]
    inner = [(i, o) for i, o in pairs if 0 < i + o < rows // 2 - 1]
    for i, o in inner:
        with_x(i, o)
    @pl.loop(1, group)
    def _(rel):
        meta_copy(rel).wait_send()
        p_copy(rel).wait_send()
        h_copy(rel, 0).wait_send()

    wait_halo_sent(0)
    wait_halo_sent(1)
    wait_halo(2)
    for i, o in pairs:
        if (i, o) not in inner:
            with_x(i, o)


    wait_halo_sent(2)


def solution(mesh):
    domains, group = mesh.shape["grid"], mesh.shape["dom"]
    side = 4

    def shards(home, p_grid, p_mask, h_grid, h_mask, x_inv, x_mask):
        rows, band, block, _ = p_grid.shape
        kind = p_grid.dtype
        two = 2 * block
        own = (rows, band, block, block)
        slots = (group, band, block, block)
        out = jax.ShapeDtypeStruct(own, kind)
        anywhere = pl.BlockSpec(memory_space=pl.ANY)
        return pl.pallas_call(
            functools.partial(kernel, domains, group, side, rows),
            out_shape=(out, out),
            in_specs=[anywhere] * 7,
            out_specs=(pl.BlockSpec(memory_space=pltpu.VMEM),) * 2,
            scratch_shapes=[
                pltpu.VMEM(own, kind),
                pltpu.VMEM(own, kind),
                pltpu.VMEM(own, kind),
                pltpu.VMEM(slots, kind),
                pltpu.VMEM(slots, kind),
                pltpu.VMEM(slots, kind),
                pltpu.VMEM((group, H_CUTS[0][1], block, block), kind),
                pltpu.VMEM((rows + 2 * P_HALO, band, block, block), kind),
                pltpu.VMEM((rows + 2 * H_HALO, band, block, block), kind),
                pltpu.VMEM((rows + 2 * X_HALO, band, block, block), kind),
                pltpu.VMEM((rows // 2, 2 * two, 5 * two), kind),
                pltpu.VMEM((two, 7 * two), kind),
                pltpu.VMEM((8, 128), jnp.int32),
                pltpu.VMEM((group, 8, 128), jnp.int32),
                pltpu.SMEM((group, 1, 128), jnp.int32),
                pltpu.SMEM((rows,), jnp.int32),
                pltpu.SMEM((rows, band), jnp.int32),
                pltpu.SMEM((rows, band), jnp.int32),
                pltpu.SMEM((rows, band), jnp.int32),
                pltpu.SemaphoreType.DMA((8,)),
                pltpu.SemaphoreType.DMA((4, group)),
                pltpu.SemaphoreType.DMA((4, group)),
                pltpu.SemaphoreType.DMA((3, 2, 5)),
                pltpu.SemaphoreType.DMA((3, 2, 5)),
            ],
            compiler_params=pltpu.CompilerParams(
                collective_id=0, has_side_effects=True, vmem_limit_bytes=51 << 20
            ),
        )(*(pltpu.with_memory_space_constraint(a, pltpu.HBM) for a in (home, p_mask, h_mask, x_mask, p_grid, h_grid, x_inv)))

    rows_spec = P(("grid", "dom"))
    return jax.shard_map(
        shards,
        mesh=mesh,
        in_specs=(rows_spec,) * 7,
        out_specs=(rows_spec, rows_spec),
        check_vma=False,
    )
```
